32 devices in a mesh: group: 2 (over y), batch: 4 (over z), expert: 4 (over x, core).
Axes of the slice: x: 2, y: 2, z: 4, core: 2. Of those that a mesh axis runs over, the one named last changes fastest.
Arguments:
- residual_in: bfloat16 [128, 4096], P(('group', 'batch')), parts along dimension 0, may hold values from -11 to 11
- queries: bfloat16 [128, 16, 128], P(('group', 'batch'), 'expert'), parts along dimension 0, may hold values from -150 to 150
- key_new: bfloat16 [128, 4, 128], P(('group', 'batch'), 'expert'), parts along dimension 0, may hold values from -6 to 6
- value_new: bfloat16 [128, 4, 128], P(('group', 'batch'), 'expert'), parts along dimension 0, may hold values from -6 to 6
- key_cache: bfloat16 [128, 4, 256, 128], P(('group', 'batch'), 'expert'), parts along dimension 0, may hold values from -6 to 6
- value_cache: bfloat16 [128, 4, 256, 128], P(('group', 'batch'), 'expert'), parts along dimension 0, may hold values from -6 to 6
- cache_len: int32 [128], P(('group', 'batch')), parts along dimension 0, may hold values from 1 to 256, 8192 in all
- new_slot: int32 [128], P(('group', 'batch')), parts along dimension 0, may hold values 0 or 1
- out_weight: bfloat16 [2048, 4096], P('expert'), may hold values from -0.125 to 0.125
- norm_gain: float32 [4096], replicated, may hold values from 0.5 to 1.5
- router: bfloat16 [4096, 4], replicated, may hold values from -0.09375 to 0.09375
- chosen: int32 [128, 2], P(('group', 'batch')), parts along dimension 0, may hold values from 0 to 3, all different within a row; in each aligned block of 16 rows (0 to 15, 16 to 31, ...) at most 12 rows name the same one
- w_gate: bfloat16 [4, 4096, 8192], P('expert', None, 'batch'), may hold values from -0.09375 to 0.09375
- w_up: bfloat16 [4, 4096, 8192], P('expert', None, 'batch'), may hold values from -0.09375 to 0.09375
- w_down: bfloat16 [4, 8192, 4096], P('expert', 'batch'), may hold values from -0.0625 to 0.0625
Outputs:
- layer_out: bfloat16 [128, 4096], P(('group', 'batch', 'expert')), parts along dimension 0
The draws below stay inside these ranges and needn't reach their ends.
There are 2 independent parts, one for each index of `group`. The reference program is written for one: setup_inputs(seed, part) draws one part's arguments, and reference() takes and returns one part's arrays. A program takes and returns all parts, laid end to end along the dimension named above; an argument that names none is the same for every part. Nothing has to cross between parts.
Inputs may be any that keep to these rules, and one draw needn't show every extreme that they name: `chosen`: each row names 2 different experts. Among the rows of one device no expert is named by more than 12 rows, and in every draw some expert is named by exactly 12 rows of some device. `cache_len`: the lengths of a part sum to 8192, and the largest is exactly 256.
All inputs are finite; a program needn't handle non-finite values. No bound on the sum of `cache_len` or of `new_slot` on one device may be relied on, other than what follows from the above.
Results may differ from the reference program's by a relative error of at most 0.017.
Values may be sent and summed in bfloat16 or wider, within the bound.
A program may use at most 128 MiB of HBM per device.

```python
import math
import jax
import jax.numpy as jnp
import numpy as np
from jax import lax

D = 4096
H = 16
KVH = 4
HD = 128
E = 4
TOP = 2
FF = 8192
SLOT_DEV = 16
CACHE = 256
CAP = 12
SLOTS = 64


def attention_parts(key):
    base = jax.random.fold_in(key, 1234)
    key_query, key_fresh, key_cached = jax.random.split(base, 3)
    queries = jnp.clip(jax.random.normal(key_query, (SLOTS, H, HD), jnp.float32), -6.0, 6.0)
    fresh_keys = jnp.clip(jax.random.normal(key_fresh, (SLOTS, KVH, HD), jnp.float32), -6.0, 6.0)
    cached = jnp.clip(jax.random.normal(key_cached, (SLOTS, KVH, CACHE, HD), jnp.float32), -6.0, 6.0)
    return (jnp.clip(queries, -150.0, 150.0), fresh_keys, cached)


def draw_queries(key, part):
    return attention_parts(key)[0].astype(jnp.bfloat16)


def draw_key_new(key, part):
    return attention_parts(key)[1].astype(jnp.bfloat16)


def draw_key_cache(key, part):
    return attention_parts(key)[2].astype(jnp.bfloat16)


def draw_residual_in(key, part):
    base = jax.random.fold_in(key, 77)
    key_drawn, key_rows, key_columns = jax.random.split(base, 3)
    drawn = jnp.clip(jax.random.normal(key_drawn, (SLOTS, D), jnp.float32), -3.0, 3.0)
    row_scale = jnp.exp(jax.random.uniform(key_rows, (SLOTS, 1), jnp.float32, jnp.log(0.1), jnp.log(1.0)))
    column_scale = jnp.exp(jax.random.uniform(key_columns, (1, D), jnp.float32, jnp.log(0.3), jnp.log(3.0)))
    return (drawn * row_scale * column_scale).astype(jnp.bfloat16)


def set_ends(entries, stream_key, smallest, largest):
    extent = entries.shape
    place = [jax.random.randint(jax.random.fold_in(stream_key, axis), (), 0, extent[axis]) for axis in range(len(extent))]
    entries = entries.at[tuple(place)].set(smallest)
    longest = extent.index(max(extent))
    place[longest] = (place[longest] + 1) % extent[longest]
    return entries.at[tuple(place)].set(largest)


def steps_of(key, extent, cuts, low, high):
    loudness, own = 1.0, jax.random.fold_in(key, 6)
    for axis_at, parts in cuts:
        heights = jnp.exp(jax.random.uniform(jax.random.fold_in(own, axis_at), (parts,), jnp.float32, low / len(cuts), high / len(cuts)))
        loudness = loudness * jnp.repeat(heights, extent[axis_at] // parts).reshape([-1 if axis == axis_at else 1 for axis in range(len(extent))])
    return loudness


def split_up(count, total, bound, lean):
    loads = [(1 << 20) // math.isqrt(standing ** lean) + 1 for standing in range(2, count + 1)]
    rest, holding = total - bound - (count - 1), [1] * (count - 1)
    while rest > 0:
        free = [i for i in range(count - 1) if holding[i] < bound]
        whole, budget = sum([loads[i] for i in free]), rest
        for i in free:
            more = min(bound - holding[i], max(1, budget * loads[i] // whole), rest)
            holding[i] = holding[i] + more
            rest = rest - more
    return np.array([bound] + holding)


def ragged(rng, amount, total, most, skew):
    if amount == 2:
        one = jax.random.randint(rng, (), max(1, total - most), min(most, total - 1) + 1)
        return jnp.stack([one, total - one])
    sizes = jnp.asarray(split_up(amount, total, most, skew), jnp.int32)
    couples = (amount - 1) // 2
    giver, sink = sizes[1:1 + 2 * couples:2], sizes[2:2 + 2 * couples:2]
    margin = jnp.minimum(giver - 1, most - sink)
    moved = jax.random.randint(jax.random.fold_in(rng, 1), (couples,), 0, 1 << 20) % (margin + 1)
    sizes = sizes.at[1:1 + 2 * couples:2].set(giver - moved).at[2:2 + 2 * couples:2].set(sink + moved)
    return sizes[jax.random.permutation(jax.random.fold_in(rng, 2), amount)]


def assign_block(rng, own, number, rows, count, top, most, skew):
    sequence = jax.random.permutation(rng, count)
    heavy_load, usual = shares(count, rows * top, most, skew, True), shares(count, rows * top, most, skew, False)
    places = jnp.arange(count)

    def named(sizes, offset_by):
        used = int((sizes > 0).sum())
        fixed = max(1, used // 4)
        shifted = fixed + (places - fixed + offset_by * (used - fixed)) % max(1, count - fixed)
        return jnp.zeros((count,), jnp.int32).at[sequence[jnp.where(places < fixed, places, shifted)]].set(jnp.asarray(sizes, jnp.int32))

    sizes = jnp.where(number % 4 == 0, named(heavy_load, number // 4), named(usual, number - number // 4 - 1))
    mixed = jax.random.permutation(jax.random.fold_in(own, 3), count)
    source_of, receiver = mixed[0:count // 2 * 2:2], mixed[1:count // 2 * 2:2]
    room = jnp.minimum(sizes[source_of] - 1, most - sizes[receiver]) // 2
    room = jnp.where((source_of == sequence[0]) | (receiver == sequence[0]) | (sizes[receiver] == 0), 0, jnp.maximum(room, 0))
    shifted = jax.random.randint(jax.random.fold_in(own, 4), (count // 2,), 0, 1 << 20) % (room + 1)
    sizes = sizes.at[source_of].add(-shifted).at[receiver].add(shifted)
    members = jnp.searchsorted(jnp.cumsum(sizes), jnp.arange(rows * top), side="right").astype(jnp.int32)
    grid = members.reshape(top, rows).T
    grid = grid[jax.random.permutation(jax.random.fold_in(own, 1), rows)]
    offset_by = jax.random.randint(jax.random.fold_in(own, 2), (rows, 1), 0, top)
    return jnp.take_along_axis(grid, (jnp.arange(top)[None, :] + offset_by) % top, axis=1)


def shares(count, total, most, lean, full):
    loads = [(1 << 20) // math.isqrt(rank ** lean) + 1 for rank in range(1, count + 1)]
    largest = most if full else min(most, max(-(-total // count), total * loads[0] // sum(loads)))
    least = 1 if total - largest >= count - 1 else 0
    counts, rest = [largest] + [least] * (count - 1), total - largest - least * (count - 1)
    while rest > 0:
        free = [i for i in range(1, count) if counts[i] < largest] or [i for i in range(1, count) if counts[i] < most]
        pool, remaining = sum([loads[i] for i in free]), rest
        for i in free:
            more = min(most - counts[i], max(1, remaining * loads[i] // pool), rest)
            counts[i] = counts[i] + more
            rest = rest - more
    return np.array(counts)


def centred(own_key, shape, deviation, bound, cuts=(), dtype=jnp.bfloat16):
    array = jax.random.normal(own_key, shape, jnp.float32) * deviation
    if len(cuts) > 0:
        array = steps_of(own_key, shape, cuts, -0.22, 0.18) * array
    return jnp.clip(array, min=-bound, max=bound).astype(dtype)


def setup_inputs(seed: int = 0, part: int = 0) -> dict:
    keys = jax.random.split(jax.random.key(seed), 16)
    part_keys = jax.random.split(jax.random.fold_in(keys[15], part), 16)
    residual_in = draw_residual_in(jax.random.fold_in(jax.random.fold_in(keys[15], part), 71), part)
    queries = draw_queries(jax.random.fold_in(jax.random.fold_in(keys[15], part), 71), part)
    key_new = draw_key_new(jax.random.fold_in(jax.random.fold_in(keys[15], part), 71), part)
    value_new = centred(part_keys[3], (SLOTS, KVH, HD), 1.0, 6.0, ((0, 4), (1, 4)))
    key_cache = draw_key_cache(jax.random.fold_in(jax.random.fold_in(keys[15], part), 71), part)
    value_cache = centred(part_keys[5], (SLOTS, KVH, CACHE, HD), 1.0, 6.0, ((0, 4), (1, 4)))
    cache_len = ragged(part_keys[6], SLOTS, SLOTS * CACHE // 2, CACHE, 2).astype(jnp.int32)
    new_slot = set_ends((jax.random.randint(part_keys[7], (SLOTS,), 0, 8) < 1).astype(jnp.int32), jax.random.fold_in(part_keys[7], 1), 0, 1)
    out_weight = centred(keys[8], (H * HD, D), (H * HD) ** -0.5, 0.125, ((0, 4),))
    norm_gain = jnp.clip(1.0 + 0.1 * jax.random.normal(keys[9], (D,), jnp.float32), 0.5, 1.5)
    router = centred(keys[10], (D, E), D ** -0.5, 0.09375)
    chosen_keys = jax.random.split(jax.random.fold_in(part_keys[11], 1), SLOTS // SLOT_DEV)
    chosen_turns = jax.random.permutation(jax.random.fold_in(part_keys[11], 3), SLOTS // SLOT_DEV)
    chosen = jax.vmap(lambda own, number: assign_block(jax.random.fold_in(part_keys[11], 2), own, number, SLOT_DEV, E, TOP, CAP, 2))(chosen_keys, chosen_turns).reshape((SLOTS, TOP))
    w_gate = centred(keys[12], (E, D, FF), D ** -0.5, 0.09375, ((0, 4), (2, 4)))
    w_up = centred(keys[13], (E, D, FF), D ** -0.5, 0.09375, ((0, 4), (2, 4)))
    w_down = centred(keys[14], (E, FF, D), FF ** -0.5, 0.0625, ((0, 4), (1, 4)))
    return {"residual_in": residual_in, "queries": queries, "key_new": key_new, "value_new": value_new, "key_cache": key_cache, "value_cache": value_cache, "cache_len": cache_len, "new_slot": new_slot, "out_weight": out_weight, "norm_gain": norm_gain, "router": router, "chosen": chosen, "w_gate": w_gate, "w_up": w_up, "w_down": w_down}


epsilon = 1e-05

def attend(queries, key_new, value_new, key_cache, value_cache, cache_len, new_slot):
    slot_count, head_count, head_width = queries.shape
    kv_count = key_cache.shape[1]
    length = key_cache.shape[2]
    group_size = head_count // kv_count
    grouped = queries.astype(jnp.float32).reshape(slot_count, kv_count, group_size, head_width)
    scaling = float(head_width) ** (-0.5)
    scores = jnp.einsum('skgd,sktd->skgt', grouped, key_cache.astype(jnp.float32)) * scaling
    own_score = jnp.einsum('skgd,skd->skg', grouped, key_new.astype(jnp.float32)) * scaling
    places = lax.broadcasted_iota(jnp.int32, (slot_count, length), 1)
    usable = (places < cache_len[:, None]) & (new_slot[:, None] == 0)
    usable = usable[:, None, None, :]
    scores = jnp.where(usable, scores, jnp.float32(-1e+30))
    highest = jnp.maximum(lax.optimization_barrier(jnp.max(scores, axis=3)), own_score)
    weights = jnp.where(usable, jnp.exp(scores - highest[..., None]), jnp.float32(0.0))
    own_weight = jnp.exp(own_score - highest)
    denominator = lax.optimization_barrier(jnp.sum(weights, axis=3)) + own_weight
    probabilities = (weights / denominator[..., None]).astype(jnp.bfloat16)
    own_prob = (own_weight / denominator).astype(jnp.bfloat16)
    attended = jnp.einsum('skgt,sktd->skgd', probabilities.astype(jnp.float32), value_cache.astype(jnp.float32))
    attended = attended + own_prob.astype(jnp.float32)[..., None] * value_new.astype(jnp.float32)[:, :, None, :]
    return attended.reshape(slot_count, head_count * head_width).astype(jnp.bfloat16)

def mixing(logits, chosen, expert_count):
    labels = lax.broadcasted_iota(jnp.int32, (1, 1, expert_count), 2)
    picking = (chosen[:, :, None] == labels).astype(jnp.float32)
    chosen_logits = lax.optimization_barrier(jnp.sum(picking * logits[:, None, :], axis=2))
    leading = jax.nn.sigmoid(chosen_logits[:, 0] - chosen_logits[:, 1])
    fractions = jnp.stack([leading, 1.0 - leading], axis=1)
    return lax.optimization_barrier(jnp.sum(picking * fractions[:, :, None], axis=1))

def reference(residual_in, queries, key_new, value_new, key_cache, value_cache, cache_len, new_slot, out_weight, norm_gain, router, chosen, w_gate, w_up, w_down):
    attended = attend(queries, key_new, value_new, key_cache, value_cache, cache_len, new_slot)
    projected = jnp.dot(attended, out_weight, preferred_element_type=jnp.float32)
    stream = (residual_in.astype(jnp.float32) + projected).astype(jnp.bfloat16)
    values = stream.astype(jnp.float32)
    scaling = lax.rsqrt(lax.optimization_barrier(jnp.mean(values * values, axis=1, keepdims=True)) + epsilon)
    normed = (values * scaling * norm_gain).astype(jnp.bfloat16)
    logits = jnp.dot(normed, router, preferred_element_type=jnp.float32)
    expert_count = router.shape[1]
    coef = mixing(logits, chosen, expert_count)
    result = values
    for expert in range(expert_count):
        gate_part = jnp.dot(normed, w_gate[expert], preferred_element_type=jnp.float32)
        up_part = jnp.dot(normed, w_up[expert], preferred_element_type=jnp.float32)
        hidden = (jax.nn.silu(gate_part) * up_part).astype(jnp.bfloat16)
        expert_out = jnp.dot(hidden, w_down[expert], preferred_element_type=jnp.float32)
        result = result + coef[:, expert:expert + 1] * expert_out
    return result.astype(jnp.bfloat16)
```

```python
import functools

import jax
import jax.numpy as jnp
from jax import lax
from jax.experimental import pallas as pl
from jax.experimental.pallas import tpu as pltpu
from jax.sharding import PartitionSpec as P

EPS = 1e-05
MESH = pl.DeviceIdType.MESH
PAD = 128


def chunk_of(extent, wanted):
    return wanted if extent % wanted == 0 else extent


def kernel(
    nb, ne,
    lens, fresh, chosen,
    resid_h, q_h, kn_h, vn_h, k_h, v_h, wo_h, gain_h, router_h, wg_h, wu_h, wd_h,
    out,
    resid, q, kn, vn, k, v, wo, gain, router, wg, wu, wd,
    scores, own, att, part, resid_rows, part_in, msg, msg_in, rows32, x, hidden,
    y, y_in, mine, z, z_in, stream_s,
    small_sem, wo_sem, gate_sem, up_sem, down_sem,
    ra_s, ra_r, ba_s, ba_r, xa_s, xa_r, ya_s, ya_r, za_s, za_r,
):
    slots, heads, width = q.shape
    length = k.shape[1]
    dim = wo.shape[1]
    hid = wg.shape[1]
    own_rows = slots // ne
    block = nb * own_rows
    g = lax.axis_index("group")
    b = lax.axis_index("batch")
    e = lax.axis_index("expert")
    wo_n, hid_n, down_n = wo_sem.shape[0], gate_sem.shape[0], down_sem.shape[0]
    wo_c, hid_c, down_c = dim // wo_n, hid // hid_n, dim // down_n

    small = [
        pltpu.make_async_copy(src, dst, small_sem.at[i])
        for i, (src, dst) in enumerate([
            (q_h, q), (kn_h, kn), (k_h.at[:, 0], k), (vn_h, vn), (v_h.at[:, 0], v),
            (resid_h, resid), (gain_h, gain), (router_h, router),
        ])
    ]
    for copy in small:
        copy.start()
    wo_copies = []
    for i in range(wo_n):
        cols = pl.ds(i * wo_c, wo_c)
        wo_copies.append(pltpu.make_async_copy(wo_h.at[:, cols], wo.at[:, cols], wo_sem.at[i]))
        wo_copies[-1].start()

    def gate_copy(i):
        cols = pl.ds(pl.multiple_of(i * hid_c, hid_c), hid_c)
        return pltpu.make_async_copy(wg_h.at[0, :, cols], wg.at[:, cols], gate_sem.at[i])

    def up_copy(i):
        cols = pl.ds(pl.multiple_of(i * hid_c, hid_c), hid_c)
        return pltpu.make_async_copy(wu_h.at[0, :, cols], wu.at[:, cols], up_sem.at[i])

    for i in range(hid_n):
        gate_copy(i).start()
        up_copy(i).start()
    down_copies = []
    for i in range(down_n):
        cols = pl.ds(i * down_c, down_c)
        down_copies.append(pltpu.make_async_copy(wd_h.at[0, :, cols], wd.at[:, cols], down_sem.at[i]))
        down_copies[-1].start()

    def expert_peer(j):
        return (g, b, lax.rem(e + j, ne))

    def batch_peer(j):
        return (g, lax.rem(b + j, nb), e)

    barrier = pltpu.get_barrier_semaphore()
    for j in range(1, ne):
        pl.semaphore_signal(barrier, inc=1, device_id=expert_peer(j), device_id_type=MESH)
    for j in range(1, nb):
        pl.semaphore_signal(barrier, inc=1, device_id=batch_peer(j), device_id_type=MESH)

    scale = float(width) ** (-0.5)
    for i in (0, 1, 2):
        small[i].wait()
    places = lax.broadcasted_iota(jnp.int32, (heads, length), 1)
    for s in range(slots):
        used = jnp.where(fresh[s] == 0, lens[s], 0)
        at = pl.ds(s * heads, heads)
        c = lax.dot_general(q[s], k[s], (((1,), (1,)), ((), ())), preferred_element_type=jnp.float32)
        scores[at, :] = jnp.where(places < used, c * scale, jnp.float32(-1e30))
        o = jnp.sum(q[s].astype(jnp.float32) * kn[s].astype(jnp.float32), axis=1, keepdims=True)
        own[at, :] = jnp.broadcast_to(o * scale, (heads, own.shape[1]))
    c = scores[...]
    o = own[:, 0:1]
    highest = jnp.maximum(jnp.max(c, axis=1, keepdims=True), o)
    weights = jnp.exp(c - highest)
    own_weight = jnp.exp(o - highest)
    total = jnp.sum(weights, axis=1, keepdims=True) + own_weight
    scores[...] = weights / total
    own[...] = jnp.broadcast_to(own_weight / total, own.shape)
    for i in (3, 4):
        small[i].wait()
    for s in range(slots):
        at = pl.ds(s * heads, heads)
        a = jnp.dot(scores[at, :].astype(jnp.bfloat16), v[s], preferred_element_type=jnp.float32)
        own_prob = own[at, :].astype(jnp.bfloat16).astype(jnp.float32)
        att[at, :] = a + own_prob * vn[s].astype(jnp.float32)
    attended = jnp.concatenate(
        [att[pl.ds(h, slots, stride=heads), :] for h in range(heads)], axis=1
    ).astype(jnp.bfloat16)

    pl.semaphore_wait(barrier, ne - 1 + nb - 1)
    for i in range(wo_n):
        wo_copies[i].wait()
        cols = pl.ds(i * wo_c, wo_c)
        p = jnp.dot(attended, wo[:, cols], preferred_element_type=jnp.float32)
        for j in range(ne):
            part[j, :, cols] = p[j * own_rows:(j + 1) * own_rows].astype(jnp.bfloat16)
    part_copies = []
    for j in range(1, ne):
        part_copies.append(pltpu.make_async_remote_copy(
            src_ref=part.at[lax.rem(e + j, ne)], dst_ref=part_in.at[j - 1],
            send_sem=ra_s.at[j - 1], recv_sem=ra_r.at[j - 1],
            device_id=expert_peer(j), device_id_type=MESH))
        part_copies[-1].start()
    for i in (5, 6, 7):
        small[i].wait()
    r32 = resid[...].astype(jnp.float32)
    for j in range(ne):
        resid_rows[j] = r32[j * own_rows:(j + 1) * own_rows]
    summed = part[e].astype(jnp.float32)
    for j in range(1, ne):
        part_copies[j - 1].wait()
        summed = summed + part_in[j - 1].astype(jnp.float32)
    values = (resid_rows[e] + summed).astype(jnp.bfloat16).astype(jnp.float32)
    stream_s[...] = values
    norm = lax.rsqrt(jnp.mean(values * values, axis=1, keepdims=True) + EPS)
    normed = (values * norm * gain[...]).astype(jnp.bfloat16)
    msg[:, 0:dim] = normed
    n32 = normed.astype(jnp.float32)
    lane = lax.broadcasted_iota(jnp.int32, (own_rows, PAD), 1)
    row = lax.broadcasted_iota(jnp.int32, (own_rows, PAD), 0)
    logits = jnp.zeros((own_rows, PAD), jnp.float32)
    for j in range(ne):
        l = jnp.sum(n32 * router[j:j + 1, :].astype(jnp.float32), axis=1, keepdims=True)
        logits = jnp.where(lane == j, l, logits)
    first = jnp.zeros((own_rows, PAD), jnp.int32)
    second = jnp.zeros((own_rows, PAD), jnp.int32)
    for i in range(own_rows):
        first = jnp.where(row == i, chosen[e * own_rows + i, 0], first)
        second = jnp.where(row == i, chosen[e * own_rows + i, 1], second)
    la = jnp.sum(jnp.where(lane == first, logits, 0.0), axis=1, keepdims=True)
    lb = jnp.sum(jnp.where(lane == second, logits, 0.0), axis=1, keepdims=True)
    ca = 1.0 / (1.0 + jnp.exp(lb - la))
    coef = jnp.where(lane == first, ca, jnp.where(lane == second, 1.0 - ca, 0.0))
    high = coef.astype(jnp.bfloat16)
    msg[:, dim:dim + PAD] = high
    msg[:, dim + PAD:dim + 2 * PAD] = (coef - high.astype(jnp.float32)).astype(jnp.bfloat16)

    msg_copies = []
    for j in range(1, nb):
        msg_copies.append(pltpu.make_async_remote_copy(
            src_ref=msg, dst_ref=msg_in.at[j - 1],
            send_sem=ba_s.at[j - 1], recv_sem=ba_r.at[j - 1],
            device_id=batch_peer(j), device_id_type=MESH))
        msg_copies[-1].start()
    rows32[0:own_rows, :] = msg[...].astype(jnp.float32)
    for j in range(1, nb):
        msg_copies[j - 1].wait()
        rows32[j * own_rows:(j + 1) * own_rows, :] = msg_in[j - 1].astype(jnp.float32)
    x[0:block, :] = rows32[...].astype(jnp.bfloat16)
    x_copies = []
    for j in range(1, ne):
        x_copies.append(pltpu.make_async_remote_copy(
            src_ref=x.at[pl.ds(0, block)], dst_ref=x.at[pl.ds(j * block, block)],
            send_sem=xa_s.at[j - 1], recv_sem=xa_r.at[j - 1],
            device_id=expert_peer(j), device_id_type=MESH))
        x_copies[-1].start()
    for copy in x_copies:
        copy.wait()

    def gate_up(i, carry):
        gate_copy(i).wait()
        up_copy(i).wait()
        cols = pl.ds(pl.multiple_of(i * hid_c, hid_c), hid_c)
        gp = jnp.dot(x[:, 0:dim], wg[:, cols], preferred_element_type=jnp.float32)
        up = jnp.dot(x[:, 0:dim], wu[:, cols], preferred_element_type=jnp.float32)
        hidden[:, cols] = (gp / (1.0 + jnp.exp(-gp)) * up).astype(jnp.bfloat16)
        return carry

    lax.fori_loop(0, hid_n, gate_up, 0)

    lanes = lax.broadcasted_iota(jnp.int32, (ne * block, PAD), 1)
    both = x[:, dim:dim + PAD].astype(jnp.float32) + x[:, dim + PAD:dim + 2 * PAD].astype(jnp.float32)
    my_coef = jnp.sum(jnp.where(lanes == e, both, 0.0), axis=1, keepdims=True)

    y_copies, z_copies = [], []

    def forward(n):
        cols = pl.ds(n * down_c, down_c)
        acc = y[n, 0:block, :].astype(jnp.float32)
        for j in range(1, ne):
            y_copies[n][j - 1].wait()
            acc = acc + y_in[n, j - 1].astype(jnp.float32)
        mine[:, cols] = acc[0:own_rows]
        sent = []
        for j in range(1, nb):
            z[n, j - 1] = acc[j * own_rows:(j + 1) * own_rows].astype(jnp.bfloat16)
        for j in range(1, nb):
            sent.append(pltpu.make_async_remote_copy(
                src_ref=z.at[n, j - 1], dst_ref=z_in.at[n, j - 1],
                send_sem=za_s.at[n, j - 1], recv_sem=za_r.at[n, j - 1],
                device_id=batch_peer(nb - j), device_id_type=MESH))
            sent[-1].start()
        z_copies.append(sent)

    def finish(n):
        cols = pl.ds(n * down_c, down_c)
        acc = stream_s[:, cols] + mine[:, cols]
        for j in range(1, nb):
            z_copies[n][j - 1].wait()
            acc = acc + z_in[n, j - 1].astype(jnp.float32)
        out[:, cols] = acc.astype(jnp.bfloat16)

    for n in range(down_n):
        cols = pl.ds(n * down_c, down_c)
        down_copies[n].wait()
        d = jnp.dot(hidden[...], wd[:, cols], preferred_element_type=jnp.float32)
        y[n] = (d * my_coef).astype(jnp.bfloat16)
        sent = []
        for j in range(1, ne):
            sent.append(pltpu.make_async_remote_copy(
                src_ref=y.at[n, pl.ds(j * block, block)], dst_ref=y_in.at[n, j - 1],
                send_sem=ya_s.at[n, j - 1], recv_sem=ya_r.at[n, j - 1],
                device_id=expert_peer(ne - j), device_id_type=MESH))
            sent[-1].start()
        y_copies.append(sent)
        if n > 0:
            forward(n - 1)
    forward(down_n - 1)
    for n in range(down_n):
        finish(n)


def body(nb, ne, residual_in, queries, key_new, value_new, key_cache, value_cache,
         cache_len, new_slot, out_weight, norm_gain, router, chosen, w_gate, w_up, w_down):
    slots, heads, width = queries.shape
    length = key_cache.shape[2]
    feat, dim = out_weight.shape
    hid = w_gate.shape[2]
    own_rows = slots // ne
    block = nb * own_rows
    wo_n = dim // chunk_of(dim, 1024)
    hid_n = hid // chunk_of(hid, 256)
    down_n = dim // chunk_of(dim, 1024)
    down_c = dim // down_n
    bf, f32 = jnp.bfloat16, jnp.float32
    smem = pl.BlockSpec(memory_space=pltpu.SMEM)
    anywhere = pl.BlockSpec(memory_space=pl.ANY)
    dma = pltpu.SemaphoreType.DMA
    ext = dim + 2 * PAD
    return pl.pallas_call(
        functools.partial(kernel, nb, ne),
        out_shape=jax.ShapeDtypeStruct((own_rows, dim), bf),
        in_specs=[smem] * 3 + [anywhere] * 12,
        out_specs=pl.BlockSpec(memory_space=pltpu.VMEM),
        scratch_shapes=[
            pltpu.VMEM((slots, dim), bf),
            pltpu.VMEM((slots, heads, width), bf),
            pltpu.VMEM((slots, 1, width), bf),
            pltpu.VMEM((slots, 1, width), bf),
            pltpu.VMEM((slots, length, width), bf),
            pltpu.VMEM((slots, length, width), bf),
            pltpu.VMEM((feat, dim), bf),
            pltpu.VMEM((1, dim), f32),
            pltpu.VMEM((ne, dim), bf),
            pltpu.VMEM((dim, hid), bf),
            pltpu.VMEM((dim, hid), bf),
            pltpu.VMEM((hid, dim), bf),
            pltpu.VMEM((slots * heads, length), f32),
            pltpu.VMEM((slots * heads, width), f32),
            pltpu.VMEM((slots * heads, width), f32),
            pltpu.VMEM((ne, own_rows, dim), bf),
            pltpu.VMEM((ne, own_rows, dim), f32),
            pltpu.VMEM((ne - 1, own_rows, dim), bf),
            pltpu.VMEM((own_rows, ext), bf),
            pltpu.VMEM((nb - 1, own_rows, ext), bf),
            pltpu.VMEM((block, ext), f32),
            pltpu.VMEM((ne * block, ext), bf),
            pltpu.VMEM((ne * block, hid), bf),
            pltpu.VMEM((down_n, ne * block, down_c), bf),
            pltpu.VMEM((down_n, ne - 1, block, down_c), bf),
            pltpu.VMEM((own_rows, dim), f32),
            pltpu.VMEM((down_n, nb - 1, own_rows, down_c), bf),
            pltpu.VMEM((down_n, nb - 1, own_rows, down_c), bf),
            pltpu.VMEM((own_rows, dim), f32),
            dma((8,)), dma((wo_n,)), dma((hid_n,)), dma((hid_n,)), dma((down_n,)),
            dma((ne - 1,)), dma((ne - 1,)), dma((nb - 1,)), dma((nb - 1,)),
            dma((ne - 1,)), dma((ne - 1,)),
            dma((down_n, ne - 1)), dma((down_n, ne - 1)),
            dma((down_n, nb - 1)), dma((down_n, nb - 1)),
        ],
        compiler_params=pltpu.CompilerParams(
            collective_id=0, has_side_effects=True, vmem_limit_bytes=67043328
        ),
    )(
        cache_len, new_slot, chosen, residual_in, queries, key_new, value_new, key_cache,
        value_cache, out_weight, norm_gain.reshape(1, dim), router.T, w_gate, w_up, w_down,
    )


def solution(mesh):
    in_specs = (
        P(("group", "batch"), None),
        P(("group", "batch"), "expert", None),
        P(("group", "batch"), "expert", None),
        P(("group", "batch"), "expert", None),
        P(("group", "batch"), "expert", None, None),
        P(("group", "batch"), "expert", None, None),
        P(("group", "batch")),
        P(("group", "batch")),
        P("expert", None),
        P(),
        P(),
        P(("group", "batch"), None),
        P("expert", None, "batch"),
        P("expert", None, "batch"),
        P("expert", "batch", None),
    )
    out_specs = P(("group", "batch", "expert"), None)
    return jax.shard_map(
        functools.partial(body, mesh.shape["batch"], mesh.shape["expert"]),
        mesh=mesh, in_specs=in_specs, out_specs=out_specs, check_vma=False,
    )
```

```python
import functools

import jax
import jax.numpy as jnp
from jax import lax
from jax.experimental import pallas as pl
from jax.experimental.pallas import tpu as pltpu
from jax.sharding import PartitionSpec as P

EPS = 1e-05
MESH = pl.DeviceIdType.MESH
PAD = 128


def chunk_of(extent, wanted):
    return wanted if extent % wanted == 0 else extent


def kernel(
    nb, ne,
    lens, fresh, chosen,
    resid_h, q_h, kn_h, vn_h, k_h, v_h, wo_h, gain_h, router_h, wg_h, wu_h, wd_h,
    out,
    resid, q, kn, vn, k, v, wo, gain, router, wg, wu, wd,
    scores, own, att, part, resid_rows, part_in, msg, msg_in, rows32, x, hidden,
    y, y_in, mine, z, z_in, stream_s,
    small_sem, wo_sem, gate_sem, up_sem, down_sem,
    ra_s, ra_r, ba_s, ba_r, xa_s, xa_r, ya_s, ya_r, za_s, za_r,
):
    slots, heads, width = q.shape
    length = k.shape[1]
    dim = wo.shape[1]
    hid = wg.shape[1]
    own_rows = slots // ne
    block = nb * own_rows
    g = lax.axis_index("group")
    b = lax.axis_index("batch")
    e = lax.axis_index("expert")
    wo_n, hid_n, down_n = wo_sem.shape[0], gate_sem.shape[0], down_sem.shape[0]
    wo_c, hid_c, down_c = dim // wo_n, hid // hid_n, dim // down_n

    small = [
        pltpu.make_async_copy(src, dst, small_sem.at[i])
        for i, (src, dst) in enumerate([
            (q_h, q), (kn_h, kn), (k_h.at[:, 0], k), (vn_h, vn), (v_h.at[:, 0], v),
            (resid_h, resid), (gain_h, gain), (router_h, router),
        ])
    ]
    for copy in small:
        copy.start()
    wo_copies = []
    for i in range(wo_n):
        cols = pl.ds(i * wo_c, wo_c)
        wo_copies.append(pltpu.make_async_copy(wo_h.at[:, cols], wo.at[:, cols], wo_sem.at[i]))
        wo_copies[-1].start()

    def gate_copy(i):
        cols = pl.ds(pl.multiple_of(i * hid_c, hid_c), hid_c)
        return pltpu.make_async_copy(wg_h.at[0, :, cols], wg.at[:, cols], gate_sem.at[i])

    def up_copy(i):
        cols = pl.ds(pl.multiple_of(i * hid_c, hid_c), hid_c)
        return pltpu.make_async_copy(wu_h.at[0, :, cols], wu.at[:, cols], up_sem.at[i])

    for i in range(hid_n):
        gate_copy(i).start(priority=1)
        up_copy(i).start(priority=1)
    down_copies = []
    for i in range(down_n):
        cols = pl.ds(i * down_c, down_c)
        down_copies.append(pltpu.make_async_copy(wd_h.at[0, :, cols], wd.at[:, cols], down_sem.at[i]))
        down_copies[-1].start(priority=1)

    def expert_peer(j):
        return (g, b, lax.rem(e + j, ne))

    def batch_peer(j):
        return (g, lax.rem(b + j, nb), e)

    barrier = pltpu.get_barrier_semaphore()
    for j in range(1, ne):
        pl.semaphore_signal(barrier, inc=1, device_id=expert_peer(j), device_id_type=MESH)
    for j in range(1, nb):
        pl.semaphore_signal(barrier, inc=1, device_id=batch_peer(j), device_id_type=MESH)

    scale = float(width) ** (-0.5)
    for i in (0, 1, 2):
        small[i].wait()
    places = lax.broadcasted_iota(jnp.int32, (heads, length), 1)
    for s in range(slots):
        used = jnp.where(fresh[s] == 0, lens[s], 0)
        at = pl.ds(s * heads, heads)
        c = lax.dot_general(q[s], k[s], (((1,), (1,)), ((), ())), preferred_element_type=jnp.float32)
        scores[at, :] = jnp.where(places < used, c * scale, jnp.float32(-1e30))
        o = jnp.sum(q[s].astype(jnp.float32) * kn[0, s:s + 1].astype(jnp.float32), axis=1, keepdims=True)
        own[at, :] = jnp.broadcast_to(o * scale, (heads, own.shape[1]))
    c = scores[...]
    o = own[:, 0:1]
    highest = jnp.maximum(jnp.max(c, axis=1, keepdims=True), o)
    weights = jnp.exp(c - highest)
    own_weight = jnp.exp(o - highest)
    total = jnp.sum(weights, axis=1, keepdims=True) + own_weight
    scores[...] = weights / total
    own[...] = jnp.broadcast_to(own_weight / total, own.shape)
    for i in (3, 4):
        small[i].wait()
    for s in range(slots):
        at = pl.ds(s * heads, heads)
        a = jnp.dot(scores[at, :].astype(jnp.bfloat16), v[s], preferred_element_type=jnp.float32)
        own_prob = own[at, :].astype(jnp.bfloat16).astype(jnp.float32)
        att[at, :] = a + own_prob * vn[0, s:s + 1].astype(jnp.float32)
    attended = jnp.concatenate(
        [att[pl.ds(h, slots, stride=heads), :] for h in range(heads)], axis=1
    ).astype(jnp.bfloat16)

    pl.semaphore_wait(barrier, ne - 1 + nb - 1)
    for i in range(wo_n):
        wo_copies[i].wait()
        cols = pl.ds(i * wo_c, wo_c)
        p = jnp.dot(attended, wo[:, cols], preferred_element_type=jnp.float32)
        for j in range(ne):
            part[j, :, cols] = p[j * own_rows:(j + 1) * own_rows].astype(jnp.bfloat16)
    part_copies = []
    for j in range(1, ne):
        part_copies.append(pltpu.make_async_remote_copy(
            src_ref=part.at[lax.rem(e + j, ne)], dst_ref=part_in.at[j - 1],
            send_sem=ra_s.at[j - 1], recv_sem=ra_r.at[j - 1],
            device_id=expert_peer(j), device_id_type=MESH))
        part_copies[-1].start()
    for i in (5, 6, 7):
        small[i].wait()
    r32 = resid[...].astype(jnp.float32)
    for j in range(ne):
        resid_rows[j] = r32[j * own_rows:(j + 1) * own_rows]
    summed = part[e].astype(jnp.float32)
    for j in range(1, ne):
        part_copies[j - 1].wait()
        summed = summed + part_in[j - 1].astype(jnp.float32)
    values = (resid_rows[e] + summed).astype(jnp.bfloat16).astype(jnp.float32)
    stream_s[...] = values
    norm = lax.rsqrt(jnp.mean(values * values, axis=1, keepdims=True) + EPS)
    normed = (values * norm * gain[...]).astype(jnp.bfloat16)
    msg[:, 0:dim] = normed
    n32 = normed.astype(jnp.float32)
    lane = lax.broadcasted_iota(jnp.int32, (own_rows, PAD), 1)
    row = lax.broadcasted_iota(jnp.int32, (own_rows, PAD), 0)
    logits = jnp.zeros((own_rows, PAD), jnp.float32)
    for j in range(ne):
        l = jnp.sum(n32 * router[j:j + 1, :].astype(jnp.float32), axis=1, keepdims=True)
        logits = jnp.where(lane == j, l, logits)
    first = jnp.zeros((own_rows, PAD), jnp.int32)
    second = jnp.zeros((own_rows, PAD), jnp.int32)
    for i in range(own_rows):
        first = jnp.where(row == i, chosen[0, e * own_rows + i], first)
        second = jnp.where(row == i, chosen[1, e * own_rows + i], second)
    la = jnp.sum(jnp.where(lane == first, logits, 0.0), axis=1, keepdims=True)
    lb = jnp.sum(jnp.where(lane == second, logits, 0.0), axis=1, keepdims=True)
    ca = 1.0 / (1.0 + jnp.exp(lb - la))
    coef = jnp.where(lane == first, ca, jnp.where(lane == second, 1.0 - ca, 0.0))
    high = coef.astype(jnp.bfloat16)
    msg[:, dim:dim + PAD] = high
    msg[:, dim + PAD:dim + 2 * PAD] = (coef - high.astype(jnp.float32)).astype(jnp.bfloat16)

    msg_copies = []
    for j in range(1, nb):
        msg_copies.append(pltpu.make_async_remote_copy(
            src_ref=msg, dst_ref=msg_in.at[j - 1],
            send_sem=ba_s.at[j - 1], recv_sem=ba_r.at[j - 1],
            device_id=batch_peer(j), device_id_type=MESH))
        msg_copies[-1].start()
    rows32[0:own_rows, :] = msg[...].astype(jnp.float32)
    for j in range(1, nb):
        msg_copies[j - 1].wait()
        rows32[j * own_rows:(j + 1) * own_rows, :] = msg_in[j - 1].astype(jnp.float32)
    x[0:block, :] = rows32[...].astype(jnp.bfloat16)
    x_copies = []
    for j in range(1, ne):
        x_copies.append(pltpu.make_async_remote_copy(
            src_ref=x.at[pl.ds(0, block)], dst_ref=x.at[pl.ds(j * block, block)],
            send_sem=xa_s.at[j - 1], recv_sem=xa_r.at[j - 1],
            device_id=expert_peer(j), device_id_type=MESH))
        x_copies[-1].start()
    for copy in x_copies:
        copy.wait()

    def gate_up(i, carry):
        gate_copy(i).wait()
        up_copy(i).wait()
        cols = pl.ds(pl.multiple_of(i * hid_c, hid_c), hid_c)
        gp = jnp.dot(x[:, 0:dim], wg[:, cols], preferred_element_type=jnp.float32)
        up = jnp.dot(x[:, 0:dim], wu[:, cols], preferred_element_type=jnp.float32)
        hidden[:, cols] = (gp / (1.0 + jnp.exp(-gp)) * up).astype(jnp.bfloat16)
        return carry

    lax.fori_loop(0, hid_n, gate_up, 0)

    lanes = lax.broadcasted_iota(jnp.int32, (ne * block, PAD), 1)
    both = x[:, dim:dim + PAD].astype(jnp.float32) + x[:, dim + PAD:dim + 2 * PAD].astype(jnp.float32)
    my_coef = jnp.sum(jnp.where(lanes == e, both, 0.0), axis=1, keepdims=True)

    y_copies, z_copies = [], []

    def forward(n):
        cols = pl.ds(n * down_c, down_c)
        acc = y[n, 0:block, :].astype(jnp.float32)
        for j in range(1, ne):
            y_copies[n][j - 1].wait()
            acc = acc + y_in[n, j - 1].astype(jnp.float32)
        mine[:, cols] = acc[0:own_rows]
        sent = []
        for j in range(1, nb):
            z[n, j - 1] = acc[j * own_rows:(j + 1) * own_rows].astype(jnp.bfloat16)
        for j in range(1, nb):
            sent.append(pltpu.make_async_remote_copy(
                src_ref=z.at[n, j - 1], dst_ref=z_in.at[n, j - 1],
                send_sem=za_s.at[n, j - 1], recv_sem=za_r.at[n, j - 1],
                device_id=batch_peer(nb - j), device_id_type=MESH))
            sent[-1].start()
        z_copies.append(sent)

    def finish(n):
        cols = pl.ds(n * down_c, down_c)
        acc = stream_s[:, cols] + mine[:, cols]
        for j in range(1, nb):
            z_copies[n][j - 1].wait()
            acc = acc + z_in[n, j - 1].astype(jnp.float32)
        out[:, cols] = acc.astype(jnp.bfloat16)

    for n in range(down_n):
        cols = pl.ds(n * down_c, down_c)
        down_copies[n].wait()
        d = jnp.dot(hidden[...], wd[:, cols], preferred_element_type=jnp.float32)
        y[n] = (d * my_coef).astype(jnp.bfloat16)
        sent = []
        for j in range(1, ne):
            sent.append(pltpu.make_async_remote_copy(
                src_ref=y.at[n, pl.ds(j * block, block)], dst_ref=y_in.at[n, j - 1],
                send_sem=ya_s.at[n, j - 1], recv_sem=ya_r.at[n, j - 1],
                device_id=expert_peer(ne - j), device_id_type=MESH))
            sent[-1].start()
        y_copies.append(sent)
        if n > 0:
            forward(n - 1)
    forward(down_n - 1)
    for n in range(down_n):
        finish(n)


def body(nb, ne, residual_in, queries, key_new, value_new, key_cache, value_cache,
         cache_len, new_slot, out_weight, norm_gain, router, chosen, w_gate, w_up, w_down):
    slots, heads, width = queries.shape
    length = key_cache.shape[2]
    feat, dim = out_weight.shape
    hid = w_gate.shape[2]
    own_rows = slots // ne
    block = nb * own_rows
    wo_n = dim // chunk_of(dim, 1024)
    hid_n = hid // chunk_of(hid, 256)
    down_n = dim // chunk_of(dim, 1024)
    down_c = dim // down_n
    bf, f32 = jnp.bfloat16, jnp.float32
    smem = pl.BlockSpec(memory_space=pltpu.SMEM)
    anywhere = pl.BlockSpec(memory_space=pl.ANY)
    dma = pltpu.SemaphoreType.DMA
    ext = dim + 2 * PAD
    return pl.pallas_call(
        functools.partial(kernel, nb, ne),
        out_shape=jax.ShapeDtypeStruct((own_rows, dim), bf),
        in_specs=[smem] * 3 + [anywhere] * 12,
        out_specs=pl.BlockSpec(memory_space=pltpu.VMEM),
        scratch_shapes=[
            pltpu.VMEM((slots, dim), bf),
            pltpu.VMEM((slots, heads, width), bf),
            pltpu.VMEM((1, slots, width), bf),
            pltpu.VMEM((1, slots, width), bf),
            pltpu.VMEM((slots, length, width), bf),
            pltpu.VMEM((slots, length, width), bf),
            pltpu.VMEM((feat, dim), bf),
            pltpu.VMEM((1, dim), f32),
            pltpu.VMEM((ne, dim), bf),
            pltpu.VMEM((dim, hid), bf),
            pltpu.VMEM((dim, hid), bf),
            pltpu.VMEM((hid, dim), bf),
            pltpu.VMEM((slots * heads, length), f32),
            pltpu.VMEM((slots * heads, width), f32),
            pltpu.VMEM((slots * heads, width), f32),
            pltpu.VMEM((ne, own_rows, dim), bf),
            pltpu.VMEM((ne, own_rows, dim), f32),
            pltpu.VMEM((ne - 1, own_rows, dim), bf),
            pltpu.VMEM((own_rows, ext), bf),
            pltpu.VMEM((nb - 1, own_rows, ext), bf),
            pltpu.VMEM((block, ext), f32),
            pltpu.VMEM((ne * block, ext), bf),
            pltpu.VMEM((ne * block, hid), bf),
            pltpu.VMEM((down_n, ne * block, down_c), bf),
            pltpu.VMEM((down_n, ne - 1, block, down_c), bf),
            pltpu.VMEM((own_rows, dim), f32),
            pltpu.VMEM((down_n, nb - 1, own_rows, down_c), bf),
            pltpu.VMEM((down_n, nb - 1, own_rows, down_c), bf),
            pltpu.VMEM((own_rows, dim), f32),
            dma((8,)), dma((wo_n,)), dma((hid_n,)), dma((hid_n,)), dma((down_n,)),
            dma((ne - 1,)), dma((ne - 1,)), dma((nb - 1,)), dma((nb - 1,)),
            dma((ne - 1,)), dma((ne - 1,)),
            dma((down_n, ne - 1)), dma((down_n, ne - 1)),
            dma((down_n, nb - 1)), dma((down_n, nb - 1)),
        ],
        compiler_params=pltpu.CompilerParams(
            collective_id=0, has_side_effects=True, vmem_limit_bytes=67043328
        ),
    )(
        cache_len, new_slot, chosen.T, residual_in, queries, jnp.transpose(key_new, (1, 0, 2)),
        jnp.transpose(value_new, (1, 0, 2)), key_cache, value_cache, out_weight, norm_gain.reshape(1, dim), router.T, w_gate, w_up, w_down,
    )


def solution(mesh):
    in_specs = (
        P(("group", "batch"), None),
        P(("group", "batch"), "expert", None),
        P(("group", "batch"), "expert", None),
        P(("group", "batch"), "expert", None),
        P(("group", "batch"), "expert", None, None),
        P(("group", "batch"), "expert", None, None),
        P(("group", "batch")),
        P(("group", "batch")),
        P("expert", None),
        P(),
        P(),
        P(("group", "batch"), None),
        P("expert", None, "batch"),
        P("expert", None, "batch"),
        P("expert", "batch", None),
    )
    out_specs = P(("group", "batch", "expert"), None)
    return jax.shard_map(
        functools.partial(body, mesh.shape["batch"], mesh.shape["expert"]),
        mesh=mesh, in_specs=in_specs, out_specs=out_specs, check_vma=False,
    )
```

```python
import functools

import jax
import jax.numpy as jnp
from jax import lax
from jax.experimental import pallas as pl
from jax.experimental.pallas import tpu as pltpu
from jax.sharding import PartitionSpec as P

EPS = 1e-05
MESH = pl.DeviceIdType.MESH
PAD = 128


def chunk_of(extent, wanted):
    return wanted if extent % wanted == 0 else extent


def kernel(
    nb, ne,
    lens, fresh, chosen,
    resid_h, q_h, kn_h, vn_h, k_h, v_h, wo_h, gain_h, router_h, wg_h, wu_h, wd_h,
    out,
    resid, q, kn, vn, k, v, wo, gain, router, wg, wu, wd,
    scores, own, att, part, resid_rows, part_in, xin, rows32, x, hidden,
    y, y_in, held, u, u_in, mine, z, z_in, stream_s,
    small_sem, wo_sem, gate_sem, up_sem, down_sem,
    ra_s, ra_r, ba_s, ba_r, xa_s, xa_r, pa_s, pa_r, ya_s, ya_r, ua_s, ua_r, za_s, za_r,
):
    slots, heads, width = q.shape
    length = k.shape[1]
    dim = wo.shape[1]
    hid = wg.shape[1]
    own_rows = slots // ne
    block = nb * own_rows
    g = lax.axis_index("group")
    b = lax.axis_index("batch")
    e = lax.axis_index("expert")
    wo_n, hid_n, down_n = wo_sem.shape[0], gate_sem.shape[0], down_sem.shape[0]
    wo_c, hid_c, down_c = dim // wo_n, hid // hid_n, dim // down_n

    small = [
        pltpu.make_async_copy(src, dst, small_sem.at[i])
        for i, (src, dst) in enumerate([
            (q_h, q), (kn_h, kn), (k_h.at[:, 0], k), (vn_h, vn), (v_h.at[:, 0], v),
            (resid_h, resid), (gain_h, gain), (router_h, router),
        ])
    ]
    for copy in small:
        copy.start()
    wo_copies = []
    for i in range(wo_n):
        cols = pl.ds(i * wo_c, wo_c)
        wo_copies.append(pltpu.make_async_copy(wo_h.at[:, cols], wo.at[:, cols], wo_sem.at[i]))
        wo_copies[-1].start()

    def gate_copy(i):
        cols = pl.ds(pl.multiple_of(i * hid_c, hid_c), hid_c)
        return pltpu.make_async_copy(wg_h.at[0, :, cols], wg.at[:, cols], gate_sem.at[i])

    def up_copy(i):
        cols = pl.ds(pl.multiple_of(i * hid_c, hid_c), hid_c)
        return pltpu.make_async_copy(wu_h.at[0, :, cols], wu.at[:, cols], up_sem.at[i])

    for i in range(hid_n):
        gate_copy(i).start(priority=1)
        up_copy(i).start(priority=1)
    down_copies = []
    for i in range(down_n):
        cols = pl.ds(i * down_c, down_c)
        down_copies.append(pltpu.make_async_copy(wd_h.at[0, :, cols], wd.at[:, cols], down_sem.at[i]))
        down_copies[-1].start(priority=1)

    low = 2 if ne % 2 == 0 else 1
    high_n = ne // low
    eh, el = e // low, lax.rem(e, low)

    def expert_peer(j):
        return (g, b, lax.rem(e + j, ne))

    def far_peer(j):
        return (g, b, lax.rem(eh + j, high_n) * low + el)

    def pair_peer():
        return (g, b, eh * low + lax.rem(el + 1, low))

    def batch_peer(j):
        return (g, lax.rem(b + j, nb), e)

    barrier = pltpu.get_barrier_semaphore()
    for j in range(1, ne):
        pl.semaphore_signal(barrier, inc=1, device_id=expert_peer(j), device_id_type=MESH)
    for j in range(1, nb):
        pl.semaphore_signal(barrier, inc=1, device_id=batch_peer(j), device_id_type=MESH)

    scale = float(width) ** (-0.5)
    for i in (0, 1, 2):
        small[i].wait()
    places = lax.broadcasted_iota(jnp.int32, (heads, length), 1)
    for s in range(slots):
        used = jnp.where(fresh[s] == 0, lens[s], 0)
        at = pl.ds(s * heads, heads)
        c = lax.dot_general(q[s], k[s], (((1,), (1,)), ((), ())), preferred_element_type=jnp.float32)
        scores[at, :] = jnp.where(places < used, c * scale, jnp.float32(-1e30))
        o = jnp.sum(q[s].astype(jnp.float32) * kn[0, s:s + 1].astype(jnp.float32), axis=1, keepdims=True)
        own[at, :] = jnp.broadcast_to(o * scale, (heads, own.shape[1]))
    c = scores[...]
    o = own[:, 0:1]
    highest = jnp.maximum(jnp.max(c, axis=1, keepdims=True), o)
    weights = jnp.exp(c - highest)
    own_weight = jnp.exp(o - highest)
    total = jnp.sum(weights, axis=1, keepdims=True) + own_weight
    scores[...] = weights / total
    own[...] = jnp.broadcast_to(own_weight / total, own.shape)
    for i in (3, 4):
        small[i].wait()
    for s in range(slots):
        at = pl.ds(s * heads, heads)
        a = jnp.dot(scores[at, :].astype(jnp.bfloat16), v[s], preferred_element_type=jnp.float32)
        own_prob = own[at, :].astype(jnp.bfloat16).astype(jnp.float32)
        att[at, :] = a + own_prob * vn[0, s:s + 1].astype(jnp.float32)
    attended = jnp.concatenate(
        [att[pl.ds(h, slots, stride=heads), :] for h in range(heads)], axis=1
    ).astype(jnp.bfloat16)

    pl.semaphore_wait(barrier, ne - 1 + nb - 1)
    part_copies = []
    for i in range(wo_n):
        wo_copies[i].wait()
        cols = pl.ds(i * wo_c, wo_c)
        p = jnp.dot(attended, wo[:, cols], preferred_element_type=jnp.float32)
        for j in range(ne):
            part[i, j] = p[j * own_rows:(j + 1) * own_rows].astype(jnp.bfloat16)
        for j in range(1, ne):
            part_copies.append(pltpu.make_async_remote_copy(
                src_ref=part.at[i, lax.rem(e + j, ne)], dst_ref=part_in.at[i, j - 1],
                send_sem=ra_s.at[i, j - 1], recv_sem=ra_r.at[i, j - 1],
                device_id=expert_peer(j), device_id_type=MESH))
            part_copies[-1].start()
    for i in (5, 6, 7):
        small[i].wait()
    r32 = resid[...].astype(jnp.float32)
    for j in range(ne):
        resid_rows[j] = r32[j * own_rows:(j + 1) * own_rows]
    for copy in part_copies:
        copy.wait()
    for i in range(wo_n):
        cols = pl.ds(i * wo_c, wo_c)
        summed = part[i, e].astype(jnp.float32)
        for j in range(1, ne):
            summed = summed + part_in[i, j - 1].astype(jnp.float32)
        stream_s[:, cols] = (resid_rows[e, :, cols] + summed).astype(jnp.bfloat16).astype(jnp.float32)
    values = stream_s[...]
    norm = lax.rsqrt(jnp.mean(values * values, axis=1, keepdims=True) + EPS)
    normed = (values * norm * gain[...]).astype(jnp.bfloat16)
    xin[0, 0, :, 0:dim] = normed
    n32 = normed.astype(jnp.float32)
    lane = lax.broadcasted_iota(jnp.int32, (own_rows, PAD), 1)
    row = lax.broadcasted_iota(jnp.int32, (own_rows, PAD), 0)
    logits = jnp.zeros((own_rows, PAD), jnp.float32)
    for j in range(ne):
        l = jnp.sum(n32 * router[j:j + 1, :].astype(jnp.float32), axis=1, keepdims=True)
        logits = jnp.where(lane == j, l, logits)
    first = jnp.zeros((own_rows, PAD), jnp.int32)
    second = jnp.zeros((own_rows, PAD), jnp.int32)
    for i in range(own_rows):
        first = jnp.where(row == i, chosen[0, e * own_rows + i], first)
        second = jnp.where(row == i, chosen[1, e * own_rows + i], second)
    la = jnp.sum(jnp.where(lane == first, logits, 0.0), axis=1, keepdims=True)
    lb = jnp.sum(jnp.where(lane == second, logits, 0.0), axis=1, keepdims=True)
    ca = 1.0 / (1.0 + jnp.exp(lb - la))
    coef = jnp.where(lane == first, ca, jnp.where(lane == second, 1.0 - ca, 0.0))
    high = coef.astype(jnp.bfloat16)
    xin[0, 0, :, dim:dim + PAD] = high
    xin[0, 0, :, dim + PAD:dim + 2 * PAD] = (coef - high.astype(jnp.float32)).astype(jnp.bfloat16)

    def take(s, k):
        at = (s * nb + k) * own_rows
        rows32[at:at + own_rows, :] = xin[s, k].astype(jnp.float32)

    def far_copy(j, k):
        return pltpu.make_async_remote_copy(
            src_ref=xin.at[0, k], dst_ref=xin.at[j, k],
            send_sem=xa_s.at[j - 1, k], recv_sem=xa_r.at[j - 1, k],
            device_id=far_peer(j), device_id_type=MESH)

    def pair_copy(j, k):
        return pltpu.make_async_remote_copy(
            src_ref=xin.at[j, k], dst_ref=xin.at[high_n + j, k],
            send_sem=pa_s.at[j, k], recv_sem=pa_r.at[j, k],
            device_id=pair_peer(), device_id_type=MESH)

    near_first = sorted(range(nb), key=lambda k: min(k, nb - k))
    z_rows = {}
    for k in near_first[1:]:
        z_rows[k] = pltpu.make_async_remote_copy(
            src_ref=xin.at[0, 0], dst_ref=xin.at[0, k],
            send_sem=ba_s.at[k - 1], recv_sem=ba_r.at[k - 1],
            device_id=batch_peer(k), device_id_type=MESH)
        z_rows[k].start()
    for k in near_first:
        if k > 0:
            z_rows[k].wait()
        for j in range(1, high_n):
            far_copy(j, k).start()
        if low == 2:
            pair_copy(0, k).start()
        take(0, k)
    for k in near_first:
        for j in range(1, high_n):
            far_copy(j, k).wait()
            if low == 2:
                pair_copy(j, k).start()
            take(j, k)
    if low == 2:
        for j in range(high_n):
            for k in near_first:
                pair_copy(j, k).wait()
                take(high_n + j, k)
    x[...] = rows32[...].astype(jnp.bfloat16)

    def gate_up(i, carry):
        gate_copy(i).wait()
        up_copy(i).wait()
        cols = pl.ds(pl.multiple_of(i * hid_c, hid_c), hid_c)
        gp = jnp.dot(x[:, 0:dim], wg[:, cols], preferred_element_type=jnp.float32)
        up = jnp.dot(x[:, 0:dim], wu[:, cols], preferred_element_type=jnp.float32)
        hidden[:, cols] = (gp / (1.0 + jnp.exp(-gp)) * up).astype(jnp.bfloat16)
        return carry

    lax.fori_loop(0, hid_n, gate_up, 0)

    lanes = lax.broadcasted_iota(jnp.int32, (ne * block, PAD), 1)
    both = x[:, dim:dim + PAD].astype(jnp.float32) + x[:, dim + PAD:dim + 2 * PAD].astype(jnp.float32)
    my_coef = jnp.sum(jnp.where(lanes == e, both, 0.0), axis=1, keepdims=True)

    y_copies, u_copies, z_copies = [], [], []
    near = high_n * block

    def far_step(n):
        acc = y[n, 0:near, :].astype(jnp.float32)
        if low == 2:
            y_copies[n].wait()
            acc = acc + y_in[n].astype(jnp.float32)
        held[n] = acc[0:block]
        sent = []
        for j in range(1, high_n):
            u[n, j - 1] = acc[j * block:(j + 1) * block].astype(jnp.bfloat16)
            sent.append(pltpu.make_async_remote_copy(
                src_ref=u.at[n, j - 1], dst_ref=u_in.at[n, j - 1],
                send_sem=ua_s.at[n, j - 1], recv_sem=ua_r.at[n, j - 1],
                device_id=far_peer(high_n - j), device_id_type=MESH))
            sent[-1].start()
        u_copies.append(sent)

    def batch_step(n):
        cols = pl.ds(n * down_c, down_c)
        acc = held[n]
        for j in range(1, high_n):
            u_copies[n][j - 1].wait()
            acc = acc + u_in[n, j - 1].astype(jnp.float32)
        mine[:, cols] = acc[0:own_rows]
        sent = {}
        for j in sorted(range(1, nb), key=lambda k: -min(k, nb - k)):
            z[n, j - 1] = acc[j * own_rows:(j + 1) * own_rows].astype(jnp.bfloat16)
            sent[j] = pltpu.make_async_remote_copy(
                src_ref=z.at[n, j - 1], dst_ref=z_in.at[n, j - 1],
                send_sem=za_s.at[n, j - 1], recv_sem=za_r.at[n, j - 1],
                device_id=batch_peer(nb - j), device_id_type=MESH)
            sent[j].start()
        z_copies.append(sent)

    def finish(n):
        cols = pl.ds(n * down_c, down_c)
        acc = stream_s[:, cols] + mine[:, cols]
        for j in range(1, nb):
            z_copies[n][j].wait()
            acc = acc + z_in[n, j - 1].astype(jnp.float32)
        out[:, cols] = acc.astype(jnp.bfloat16)

    for n in range(down_n):
        cols = pl.ds(n * down_c, down_c)
        down_copies[n].wait()
        d = jnp.dot(hidden[...], wd[:, cols], preferred_element_type=jnp.float32)
        y[n] = (d * my_coef).astype(jnp.bfloat16)
        if low == 2:
            y_copies.append(pltpu.make_async_remote_copy(
                src_ref=y.at[n, pl.ds(near, near)], dst_ref=y_in.at[n],
                send_sem=ya_s.at[n], recv_sem=ya_r.at[n],
                device_id=pair_peer(), device_id_type=MESH))
            y_copies[-1].start()
        if n > 0:
            far_step(n - 1)
        if n > 1:
            batch_step(n - 2)
    far_step(down_n - 1)
    for n in range(max(down_n - 2, 0), down_n):
        batch_step(n)
    for n in range(down_n):
        finish(n)


def body(nb, ne, residual_in, queries, key_new, value_new, key_cache, value_cache,
         cache_len, new_slot, out_weight, norm_gain, router, chosen, w_gate, w_up, w_down):
    slots, heads, width = queries.shape
    length = key_cache.shape[2]
    feat, dim = out_weight.shape
    hid = w_gate.shape[2]
    own_rows = slots // ne
    block = nb * own_rows
    high_n = ne // 2 if ne % 2 == 0 else ne
    wo_n = dim // chunk_of(dim, 1024)
    hid_n = hid // chunk_of(hid, 256)
    down_n = dim // chunk_of(dim, 1024)
    down_c = dim // down_n
    bf, f32 = jnp.bfloat16, jnp.float32
    smem = pl.BlockSpec(memory_space=pltpu.SMEM)
    anywhere = pl.BlockSpec(memory_space=pl.ANY)
    dma = pltpu.SemaphoreType.DMA
    ext = dim + 2 * PAD
    return pl.pallas_call(
        functools.partial(kernel, nb, ne),
        out_shape=jax.ShapeDtypeStruct((own_rows, dim), bf),
        in_specs=[smem] * 3 + [anywhere] * 12,
        out_specs=pl.BlockSpec(memory_space=pltpu.VMEM),
        scratch_shapes=[
            pltpu.VMEM((slots, dim), bf),
            pltpu.VMEM((slots, heads, width), bf),
            pltpu.VMEM((1, slots, width), bf),
            pltpu.VMEM((1, slots, width), bf),
            pltpu.VMEM((slots, length, width), bf),
            pltpu.VMEM((slots, length, width), bf),
            pltpu.VMEM((feat, dim), bf),
            pltpu.VMEM((1, dim), f32),
            pltpu.VMEM((ne, dim), bf),
            pltpu.VMEM((dim, hid), bf),
            pltpu.VMEM((dim, hid), bf),
            pltpu.VMEM((hid, dim), bf),
            pltpu.VMEM((slots * heads, length), f32),
            pltpu.VMEM((slots * heads, width), f32),
            pltpu.VMEM((slots * heads, width), f32),
            pltpu.VMEM((wo_n, ne, own_rows, dim // wo_n), bf),
            pltpu.VMEM((ne, own_rows, dim), f32),
            pltpu.VMEM((wo_n, ne - 1, own_rows, dim // wo_n), bf),
            pltpu.VMEM((ne, nb, own_rows, ext), bf),
            pltpu.VMEM((ne * block, ext), f32),
            pltpu.VMEM((ne * block, ext), bf),
            pltpu.VMEM((ne * block, hid), bf),
            pltpu.VMEM((down_n, ne * block, down_c), bf),
            pltpu.VMEM((down_n, high_n * block, down_c), bf),
            pltpu.VMEM((down_n, block, down_c), f32),
            pltpu.VMEM((down_n, high_n, block, down_c), bf),
            pltpu.VMEM((down_n, high_n, block, down_c), bf),
            pltpu.VMEM((own_rows, dim), f32),
            pltpu.VMEM((down_n, nb - 1, own_rows, down_c), bf),
            pltpu.VMEM((down_n, nb - 1, own_rows, down_c), bf),
            pltpu.VMEM((own_rows, dim), f32),
            dma((8,)), dma((wo_n,)), dma((hid_n,)), dma((hid_n,)), dma((down_n,)),
            dma((wo_n, ne - 1)), dma((wo_n, ne - 1)), dma((nb - 1,)), dma((nb - 1,)),
            dma((high_n, nb)), dma((high_n, nb)), dma((high_n, nb)), dma((high_n, nb)),
            dma((down_n,)), dma((down_n,)), dma((down_n, high_n)), dma((down_n, high_n)),
            dma((down_n, nb - 1)), dma((down_n, nb - 1)),
        ],
        compiler_params=pltpu.CompilerParams(
            collective_id=0, has_side_effects=True, vmem_limit_bytes=67043328
        ),
    )(
        cache_len, new_slot, chosen.T, residual_in, queries, jnp.transpose(key_new, (1, 0, 2)),
        jnp.transpose(value_new, (1, 0, 2)), key_cache, value_cache, out_weight, norm_gain.reshape(1, dim), router.T, w_gate, w_up, w_down,
    )


def solution(mesh):
    in_specs = (
        P(("group", "batch"), None),
        P(("group", "batch"), "expert", None),
        P(("group", "batch"), "expert", None),
        P(("group", "batch"), "expert", None),
        P(("group", "batch"), "expert", None, None),
        P(("group", "batch"), "expert", None, None),
        P(("group", "batch")),
        P(("group", "batch")),
        P("expert", None),
        P(),
        P(),
        P(("group", "batch"), None),
        P("expert", None, "batch"),
        P("expert", None, "batch"),
        P("expert", "batch", None),
    )
    out_specs = P(("group", "batch", "expert"), None)
    return jax.shard_map(
        functools.partial(body, mesh.shape["batch"], mesh.shape["expert"]),
        mesh=mesh, in_specs=in_specs, out_specs=out_specs, check_vma=False,
    )
```

```python
import functools

import jax
import jax.numpy as jnp
from jax import lax
from jax.experimental import pallas as pl
from jax.experimental.pallas import tpu as pltpu
from jax.sharding import PartitionSpec as P

EPS = 1e-05
MESH = pl.DeviceIdType.MESH
PAD = 128


def chunk_of(extent, wanted):
    return wanted if extent % wanted == 0 else extent


def kernel(
    nb, ne,
    lens, fresh, chosen,
    resid_h, q_h, kn_h, vn_h, k_h, v_h, wo_h, gain_h, router_h, wg_h, wu_h, wd_h,
    out,
    resid, q, kn, vn, k, v, wo, gain, router, wg, wu, wd,
    scores, own, att, part, resid_rows, part_in, xin, rows32, x, hidden,
    y, y_in, held, u, u_in, mine, z, z_in, stream_s,
    small_sem, wo_sem, gate_sem, up_sem, down_sem,
    ra_s, ra_r, ba_s, ba_r, xa_s, xa_r, pa_s, pa_r, ya_s, ya_r, ua_s, ua_r, za_s, za_r,
):
    slots, heads, width = q.shape
    length = k.shape[1]
    dim = wo.shape[1]
    hid = wg.shape[1]
    own_rows = slots // ne
    block = nb * own_rows
    g = lax.axis_index("group")
    b = lax.axis_index("batch")
    e = lax.axis_index("expert")
    wo_n, hid_n, down_n = wo_sem.shape[0], gate_sem.shape[0], down_sem.shape[0]
    wo_c, hid_c, down_c = dim // wo_n, hid // hid_n, dim // down_n

    small = [
        pltpu.make_async_copy(src, dst, small_sem.at[i])
        for i, (src, dst) in enumerate([
            (q_h, q), (kn_h, kn), (k_h.at[:, 0], k), (vn_h, vn), (v_h.at[:, 0], v),
            (resid_h, resid), (gain_h, gain), (router_h, router),
        ])
    ]
    for copy in small:
        copy.start()
    wo_copies = []
    for i in range(wo_n):
        cols = pl.ds(i * wo_c, wo_c)
        wo_copies.append(pltpu.make_async_copy(wo_h.at[:, cols], wo.at[:, cols], wo_sem.at[i]))
        wo_copies[-1].start()

    def gate_copy(i):
        cols = pl.ds(pl.multiple_of(i * hid_c, hid_c), hid_c)
        return pltpu.make_async_copy(wg_h.at[0, :, cols], wg.at[:, cols], gate_sem.at[i])

    def up_copy(i):
        cols = pl.ds(pl.multiple_of(i * hid_c, hid_c), hid_c)
        return pltpu.make_async_copy(wu_h.at[0, :, cols], wu.at[:, cols], up_sem.at[i])

    for i in range(hid_n):
        gate_copy(i).start(priority=1)
        up_copy(i).start(priority=1)
    down_copies = []
    for i in range(down_n):
        cols = pl.ds(i * down_c, down_c)
        down_copies.append(pltpu.make_async_copy(wd_h.at[0, :, cols], wd.at[:, cols], down_sem.at[i]))
        down_copies[-1].start(priority=1)

    low = 2 if ne % 2 == 0 else 1
    high_n = ne // low
    eh, el = e // low, lax.rem(e, low)

    def expert_peer(j):
        return (g, b, lax.rem(e + j, ne))

    def far_peer(j):
        return (g, b, lax.rem(eh + j, high_n) * low + el)

    def pair_peer():
        return (g, b, eh * low + lax.rem(el + 1, low))

    def batch_peer(j):
        return (g, lax.rem(b + j, nb), e)

    barrier = pltpu.get_barrier_semaphore()
    for j in range(1, ne):
        pl.semaphore_signal(barrier, inc=1, device_id=expert_peer(j), device_id_type=MESH)
    for j in range(1, nb):
        pl.semaphore_signal(barrier, inc=1, device_id=batch_peer(j), device_id_type=MESH)

    scale = float(width) ** (-0.5)
    for i in (0, 1, 2):
        small[i].wait()
    places = lax.broadcasted_iota(jnp.int32, (heads, length), 1)
    for s in range(slots):
        used = jnp.where(fresh[s] == 0, lens[s], 0)
        at = pl.ds(s * heads, heads)
        c = lax.dot_general(q[s], k[s], (((1,), (1,)), ((), ())), preferred_element_type=jnp.float32)
        scores[at, :] = jnp.where(places < used, c * scale, jnp.float32(-1e30))
        o = jnp.sum(q[s].astype(jnp.float32) * kn[0, s:s + 1].astype(jnp.float32), axis=1, keepdims=True)
        own[at, :] = jnp.broadcast_to(o * scale, (heads, own.shape[1]))
    c = scores[...]
    o = own[:, 0:1]
    highest = jnp.maximum(jnp.max(c, axis=1, keepdims=True), o)
    weights = jnp.exp(c - highest)
    own_weight = jnp.exp(o - highest)
    total = jnp.sum(weights, axis=1, keepdims=True) + own_weight
    scores[...] = weights / total
    own[...] = jnp.broadcast_to(own_weight / total, own.shape)
    for i in (3, 4):
        small[i].wait()
    for s in range(slots):
        at = pl.ds(s * heads, heads)
        a = jnp.dot(scores[at, :].astype(jnp.bfloat16), v[s], preferred_element_type=jnp.float32)
        own_prob = own[at, :].astype(jnp.bfloat16).astype(jnp.float32)
        att[at, :] = a + own_prob * vn[0, s:s + 1].astype(jnp.float32)
    attended = jnp.concatenate(
        [att[pl.ds(h, slots, stride=heads), :] for h in range(heads)], axis=1
    ).astype(jnp.bfloat16)

    pl.semaphore_wait(barrier, ne - 1 + nb - 1)
    part_copies = []
    for i in range(wo_n):
        wo_copies[i].wait()
        cols = pl.ds(i * wo_c, wo_c)
        p = jnp.dot(attended, wo[:, cols], preferred_element_type=jnp.float32)
        for j in range(ne):
            part[i, j] = p[j * own_rows:(j + 1) * own_rows].astype(jnp.bfloat16)
        for j in range(1, ne):
            part_copies.append(pltpu.make_async_remote_copy(
                src_ref=part.at[i, lax.rem(e + j, ne)], dst_ref=part_in.at[i, j - 1],
                send_sem=ra_s.at[i, j - 1], recv_sem=ra_r.at[i, j - 1],
                device_id=expert_peer(j), device_id_type=MESH))
            part_copies[-1].start()
    for i in (5, 6, 7):
        small[i].wait()
    r32 = resid[...].astype(jnp.float32)
    for j in range(ne):
        resid_rows[j] = r32[j * own_rows:(j + 1) * own_rows]
    for copy in part_copies:
        copy.wait()
    for i in range(wo_n):
        cols = pl.ds(i * wo_c, wo_c)
        summed = part[i, e].astype(jnp.float32)
        for j in range(1, ne):
            summed = summed + part_in[i, j - 1].astype(jnp.float32)
        stream_s[:, cols] = (resid_rows[e, :, cols] + summed).astype(jnp.bfloat16).astype(jnp.float32)
    values = stream_s[...]
    norm = lax.rsqrt(jnp.mean(values * values, axis=1, keepdims=True) + EPS)
    normed = (values * norm * gain[...]).astype(jnp.bfloat16)
    xin[0, 0, :, 0:dim] = normed
    n32 = normed.astype(jnp.float32)
    lane = lax.broadcasted_iota(jnp.int32, (own_rows, PAD), 1)
    row = lax.broadcasted_iota(jnp.int32, (own_rows, PAD), 0)
    logits = jnp.zeros((own_rows, PAD), jnp.float32)
    for j in range(ne):
        l = jnp.sum(n32 * router[j:j + 1, :].astype(jnp.float32), axis=1, keepdims=True)
        logits = jnp.where(lane == j, l, logits)
    first = jnp.zeros((own_rows, PAD), jnp.int32)
    second = jnp.zeros((own_rows, PAD), jnp.int32)
    for i in range(own_rows):
        first = jnp.where(row == i, chosen[0, e * own_rows + i], first)
        second = jnp.where(row == i, chosen[1, e * own_rows + i], second)
    la = jnp.sum(jnp.where(lane == first, logits, 0.0), axis=1, keepdims=True)
    lb = jnp.sum(jnp.where(lane == second, logits, 0.0), axis=1, keepdims=True)
    ca = 1.0 / (1.0 + jnp.exp(lb - la))
    coef = jnp.where(lane == first, ca, jnp.where(lane == second, 1.0 - ca, 0.0))
    high = coef.astype(jnp.bfloat16)
    xin[0, 0, :, dim:dim + PAD] = high
    xin[0, 0, :, dim + PAD:dim + 2 * PAD] = (coef - high.astype(jnp.float32)).astype(jnp.bfloat16)

    def take(s, k):
        at = (s * nb + k) * own_rows
        rows32[at:at + own_rows, :] = xin[s, k].astype(jnp.float32)

    def far_copy(j, k):
        return pltpu.make_async_remote_copy(
            src_ref=xin.at[0, k], dst_ref=xin.at[j, k],
            send_sem=xa_s.at[j - 1, k], recv_sem=xa_r.at[j - 1, k],
            device_id=far_peer(j), device_id_type=MESH)

    def pair_copy(j, k):
        return pltpu.make_async_remote_copy(
            src_ref=xin.at[j, k], dst_ref=xin.at[high_n + j, k],
            send_sem=pa_s.at[j, k], recv_sem=pa_r.at[j, k],
            device_id=pair_peer(), device_id_type=MESH)

    near_first = sorted(range(nb), key=lambda k: min(k, nb - k))
    z_rows = {}
    for k in near_first[1:]:
        z_rows[k] = pltpu.make_async_remote_copy(
            src_ref=xin.at[0, 0], dst_ref=xin.at[0, k],
            send_sem=ba_s.at[k - 1], recv_sem=ba_r.at[k - 1],
            device_id=batch_peer(k), device_id_type=MESH)
        z_rows[k].start()
    for k in near_first:
        if k > 0:
            z_rows[k].wait()
        for j in range(1, high_n):
            far_copy(j, k).start()
        if low == 2:
            pair_copy(0, k).start()
        take(0, k)
    for k in near_first:
        for j in range(1, high_n):
            far_copy(j, k).wait()
            if low == 2:
                pair_copy(j, k).start()
            take(j, k)
    if low == 2:
        for j in range(high_n):
            for k in near_first:
                pair_copy(j, k).wait()
                take(high_n + j, k)
    x[...] = rows32[...].astype(jnp.bfloat16)

    def gate_up(i, carry):
        gate_copy(i).wait()
        up_copy(i).wait()
        cols = pl.ds(pl.multiple_of(i * hid_c, hid_c), hid_c)
        gp = jnp.dot(x[:, 0:dim], wg[:, cols], preferred_element_type=jnp.float32)
        up = jnp.dot(x[:, 0:dim], wu[:, cols], preferred_element_type=jnp.float32)
        hidden[:, cols] = (gp / (1.0 + jnp.exp(-gp)) * up).astype(jnp.bfloat16)
        return carry

    lax.fori_loop(0, hid_n, gate_up, 0)

    lanes = lax.broadcasted_iota(jnp.int32, (ne * block, PAD), 1)
    both = x[:, dim:dim + PAD].astype(jnp.float32) + x[:, dim + PAD:dim + 2 * PAD].astype(jnp.float32)
    my_coef = jnp.sum(jnp.where(lanes == e, both, 0.0), axis=1, keepdims=True)

    y_copies, u_copies, z_copies = [], [], []
    near = high_n * block

    def far_step(n):
        acc = y[n, 0:near, :].astype(jnp.float32)
        if low == 2:
            y_copies[n].wait()
            acc = acc + y_in[n].astype(jnp.float32)
        held[n] = acc[0:block]
        sent = []
        for j in range(1, high_n):
            u[n, j - 1] = acc[j * block:(j + 1) * block].astype(jnp.bfloat16)
            sent.append(pltpu.make_async_remote_copy(
                src_ref=u.at[n, j - 1], dst_ref=u_in.at[n, j - 1],
                send_sem=ua_s.at[n, j - 1], recv_sem=ua_r.at[n, j - 1],
                device_id=far_peer(high_n - j), device_id_type=MESH))
            sent[-1].start()
        u_copies.append(sent)

    def batch_step(n):
        cols = pl.ds(n * down_c, down_c)
        acc = held[n]
        for j in range(1, high_n):
            u_copies[n][j - 1].wait()
            acc = acc + u_in[n, j - 1].astype(jnp.float32)
        mine[:, cols] = acc[0:own_rows]
        sent = {}
        for j in sorted(range(1, nb), key=lambda k: -min(k, nb - k)):
            z[n, j - 1] = acc[j * own_rows:(j + 1) * own_rows].astype(jnp.bfloat16)
            sent[j] = pltpu.make_async_remote_copy(
                src_ref=z.at[n, j - 1], dst_ref=z_in.at[n, j - 1],
                send_sem=za_s.at[n, j - 1], recv_sem=za_r.at[n, j - 1],
                device_id=batch_peer(nb - j), device_id_type=MESH)
            sent[j].start()
        z_copies.append(sent)

    def finish(n):
        cols = pl.ds(n * down_c, down_c)
        acc = stream_s[:, cols] + mine[:, cols]
        for j in range(1, nb):
            z_copies[n][j].wait()
            acc = acc + z_in[n, j - 1].astype(jnp.float32)
        out[:, cols] = acc.astype(jnp.bfloat16)

    for n in range(down_n):
        cols = pl.ds(n * down_c, down_c)
        down_copies[n].wait()
        d = jnp.dot(hidden[...], wd[:, cols], preferred_element_type=jnp.float32)
        y[n] = (d * my_coef).astype(jnp.bfloat16)
        if low == 2:
            y_copies.append(pltpu.make_async_remote_copy(
                src_ref=y.at[n, pl.ds(near, near)], dst_ref=y_in.at[n],
                send_sem=ya_s.at[n], recv_sem=ya_r.at[n],
                device_id=pair_peer(), device_id_type=MESH))
            y_copies[-1].start()
        if n > 0:
            far_step(n - 1)
        if n > 1:
            batch_step(n - 2)
    far_step(down_n - 1)
    for n in range(max(down_n - 2, 0), down_n):
        batch_step(n)
    for n in range(down_n):
        finish(n)


def body(nb, ne, residual_in, queries, key_new, value_new, key_cache, value_cache,
         cache_len, new_slot, out_weight, norm_gain, router, chosen, w_gate, w_up, w_down):
    slots, heads, width = queries.shape
    length = key_cache.shape[2]
    feat, dim = out_weight.shape
    hid = w_gate.shape[2]
    own_rows = slots // ne
    block = nb * own_rows
    high_n = ne // 2 if ne % 2 == 0 else ne
    wo_n = dim // chunk_of(dim, 2048)
    hid_n = hid // chunk_of(hid, 512)
    down_n = dim // chunk_of(dim, 2048)
    down_c = dim // down_n
    bf, f32 = jnp.bfloat16, jnp.float32
    smem = pl.BlockSpec(memory_space=pltpu.SMEM)
    anywhere = pl.BlockSpec(memory_space=pl.ANY)
    dma = pltpu.SemaphoreType.DMA
    ext = dim + 2 * PAD
    return pl.pallas_call(
        functools.partial(kernel, nb, ne),
        out_shape=jax.ShapeDtypeStruct((own_rows, dim), bf),
        in_specs=[smem] * 3 + [anywhere] * 12,
        out_specs=pl.BlockSpec(memory_space=pltpu.VMEM),
        scratch_shapes=[
            pltpu.VMEM((slots, dim), bf),
            pltpu.VMEM((slots, heads, width), bf),
            pltpu.VMEM((1, slots, width), bf),
            pltpu.VMEM((1, slots, width), bf),
            pltpu.VMEM((slots, length, width), bf),
            pltpu.VMEM((slots, length, width), bf),
            pltpu.VMEM((feat, dim), bf),
            pltpu.VMEM((1, dim), f32),
            pltpu.VMEM((ne, dim), bf),
            pltpu.VMEM((dim, hid), bf),
            pltpu.VMEM((dim, hid), bf),
            pltpu.VMEM((hid, dim), bf),
            pltpu.VMEM((slots * heads, length), f32),
            pltpu.VMEM((slots * heads, width), f32),
            pltpu.VMEM((slots * heads, width), f32),
            pltpu.VMEM((wo_n, ne, own_rows, dim // wo_n), bf),
            pltpu.VMEM((ne, own_rows, dim), f32),
            pltpu.VMEM((wo_n, ne - 1, own_rows, dim // wo_n), bf),
            pltpu.VMEM((ne, nb, own_rows, ext), bf),
            pltpu.VMEM((ne * block, ext), f32),
            pltpu.VMEM((ne * block, ext), bf),
            pltpu.VMEM((ne * block, hid), bf),
            pltpu.VMEM((down_n, ne * block, down_c), bf),
            pltpu.VMEM((down_n, high_n * block, down_c), bf),
            pltpu.VMEM((down_n, block, down_c), f32),
            pltpu.VMEM((down_n, high_n, block, down_c), bf),
            pltpu.VMEM((down_n, high_n, block, down_c), bf),
            pltpu.VMEM((own_rows, dim), f32),
            pltpu.VMEM((down_n, nb - 1, own_rows, down_c), bf),
            pltpu.VMEM((down_n, nb - 1, own_rows, down_c), bf),
            pltpu.VMEM((own_rows, dim), f32),
            dma((8,)), dma((wo_n,)), dma((hid_n,)), dma((hid_n,)), dma((down_n,)),
            dma((wo_n, ne - 1)), dma((wo_n, ne - 1)), dma((nb - 1,)), dma((nb - 1,)),
            dma((high_n, nb)), dma((high_n, nb)), dma((high_n, nb)), dma((high_n, nb)),
            dma((down_n,)), dma((down_n,)), dma((down_n, high_n)), dma((down_n, high_n)),
            dma((down_n, nb - 1)), dma((down_n, nb - 1)),
        ],
        compiler_params=pltpu.CompilerParams(
            collective_id=0, has_side_effects=True, vmem_limit_bytes=67043328
        ),
    )(
        cache_len, new_slot, chosen.T, residual_in, queries, jnp.transpose(key_new, (1, 0, 2)),
        jnp.transpose(value_new, (1, 0, 2)), key_cache, value_cache, out_weight, norm_gain.reshape(1, dim), router.T, w_gate, w_up, w_down,
    )


def solution(mesh):
    in_specs = (
        P(("group", "batch"), None),
        P(("group", "batch"), "expert", None),
        P(("group", "batch"), "expert", None),
        P(("group", "batch"), "expert", None),
        P(("group", "batch"), "expert", None, None),
        P(("group", "batch"), "expert", None, None),
        P(("group", "batch")),
        P(("group", "batch")),
        P("expert", None),
        P(),
        P(),
        P(("group", "batch"), None),
        P("expert", None, "batch"),
        P("expert", None, "batch"),
        P("expert", "batch", None),
    )
    out_specs = P(("group", "batch", "expert"), None)
    return jax.shard_map(
        functools.partial(body, mesh.shape["batch"], mesh.shape["expert"]),
        mesh=mesh, in_specs=in_specs, out_specs=out_specs, check_vma=False,
    )
```
